128 devices in a mesh: group: 4 (over x), slab: 32 (over z, y, core).
Axes of the slice: x: 4, y: 4, z: 4, core: 2. Of those that a mesh axis runs over, the one named last changes fastest.
Arguments:
- queries: float32 [512, 1024], P(('group', 'slab')), may hold values from -6 to 6
- probes: int32 [512, 32], P(('group', 'slab')), may hold values from 0 to 511, all different within a row; in each aligned block of 4 rows (0 to 3, 4 to 7, ...) at most 2 rows name the same one
- codes: bfloat16 [512, 2048, 1024], P(('group', 'slab')), may hold values from 0 to 255, as said below
- scale: float32 [512, 1024], P(('group', 'slab')), may hold values from 4e-05 to 0.00032
- offset: float32 [512, 1024], P(('group', 'slab')), may hold values from -0.5 to 0.5
- tile_counts: int32 [512], P(('group', 'slab')), may hold values from 1 to 8, 2304 in all
- raw_vectors: float32 [131072, 1024], P(('group', 'slab')), may hold values from -0.5 to 0.5
- candidates: int32 [512, 64], P(('group', 'slab')), may hold values from 0 to 131071, as said below
Outputs:
- list_best: float32 [512, 32], P(('group', 'slab'))
- rerank: float32 [512, 64], P(('group', 'slab'))
The draws below stay inside these ranges and needn't reach their ends.
Inputs may be any that keep to these rules, and one draw needn't show every extreme that they name: `probes`: each query names 32 different lists; among the 4 queries of one device no list is named by more than 2 queries. List l is held by device l // 4 in the order of group+slab. `tile_counts`: some list uses all 8 tiles. `codes`: every entry is a whole number, an 8-bit level. `candidates`: vector v is stored on device v // 1024 in the order of group+slab. Among the ids of one device's queries at most 4 lie on any one device, and exactly 4 on some device.
All inputs are finite; a program needn't handle non-finite values. No bound on the sum of `tile_counts` on one device may be relied on, other than what follows from the above.
Results may differ from the reference program's by a relative error of at most 0.0013.
Values sent between devices are 32-bit elements; how exact they have to be, the bound alone decides.
No kernel may reach another device: no remote copies, remote signals or barrier semaphores. Data moves between devices by JAX's collectives and lax.ppermute only.
A program may use at most 128 MiB of HBM per device.

```python
import math
import jax
import jax.numpy as jnp
import numpy as np
from jax import lax

D = 1024
PROBE = 32
CAND = 64
Q_DEV = 4
TILES = 8
TILE = 256
V_DEV = 1024
LISTS = 512
ROWS = 2048
NQ = 512
VECS = 131072
MOST = 2
CAP = 4
N_GROUP = 4
N_SLAB = 32


def draw_codes(key, part):
    levels = jax.random.randint(jax.random.fold_in(key, 11), (LISTS, ROWS, D), 0, 256)
    return levels.astype(jnp.float32).astype(jnp.bfloat16)


def draw_candidates(key, part):
    stores = VECS // V_DEV
    entries = Q_DEV * CAND
    blocks = NQ // Q_DEV

    def one_block(block_key):
        first_key, second_key, third_key, fourth_key = jax.random.split(block_key, 4)
        full_owner = jax.random.randint(first_key, (), 0, stores)
        shuffled = jax.random.permutation(second_key, stores * CAP).astype(jnp.int32)
        priority = jnp.where(shuffled // CAP == full_owner, 0, 1).astype(jnp.int32)
        order_idx = jnp.argsort(priority, stable=True)
        chosen = shuffled[order_idx][:entries]
        chosen = jax.random.permutation(third_key, chosen)
        owners = chosen // CAP
        local_row = jax.random.randint(fourth_key, (entries,), 0, V_DEV)
        return (owners * V_DEV + local_row).astype(jnp.int32)
    block_keys = jax.random.split(jax.random.fold_in(key, 7), blocks)
    vector_ids = jax.vmap(one_block)(block_keys)
    return vector_ids.reshape(NQ, CAND).astype(jnp.int32)


def block_scale(key, shape, pieces, least, top_value):
    gain, own = 1.0, jax.random.fold_in(key, 6)
    for axis_at, parts in pieces:
        steps = jnp.exp(jax.random.uniform(jax.random.fold_in(own, axis_at), (parts,), jnp.float32, least / len(pieces), top_value / len(pieces)))
        gain = gain * jnp.repeat(steps, shape[axis_at] // parts).reshape([-1 if axis == axis_at else 1 for axis in range(len(shape))])
    return gain


def profile(number_of, total, most, lean):
    loads = [(1 << 20) // math.isqrt(grade ** lean) + 1 for grade in range(2, number_of + 1)]
    spare, counts = total - most - (number_of - 1), [1] * (number_of - 1)
    while spare > 0:
        movable = [i for i in range(number_of - 1) if counts[i] < most]
        mass, budget = sum([loads[i] for i in movable]), spare
        for i in movable:
            more = min(most - counts[i], max(1, budget * loads[i] // mass), spare)
            counts[i] = counts[i] + more
            spare = spare - more
    return np.array([most] + counts)


def ragged(own_key, count, total, most, lean):
    if count == 2:
        one = jax.random.randint(own_key, (), max(1, total - most), min(most, total - 1) + 1)
        return jnp.stack([one, total - one])
    sizes = jnp.asarray(profile(count, total, most, lean), jnp.int32)
    couples = (count - 1) // 2
    source_of, sink = sizes[1:1 + 2 * couples:2], sizes[2:2 + 2 * couples:2]
    margin = jnp.minimum(source_of - 1, most - sink)
    passed = jax.random.randint(jax.random.fold_in(own_key, 1), (couples,), 0, 1 << 20) % (margin + 1)
    sizes = sizes.at[1:1 + 2 * couples:2].set(source_of - passed).at[2:2 + 2 * couples:2].set(sink + passed)
    return sizes[jax.random.permutation(jax.random.fold_in(own_key, 2), count)]


def assign_block(rng, own, number, rows, number_of, top, bound, skew):
    ranking = jax.random.permutation(rng, number_of)
    crowded, ordinary = load_shares(number_of, rows * top, bound, skew, True), load_shares(number_of, rows * top, bound, skew, False)
    places = jnp.arange(number_of)

    def named(lengths, rotation):
        used = int((lengths > 0).sum())
        fixed = max(1, used // 4)
        passed = fixed + (places - fixed + rotation * (used - fixed)) % max(1, number_of - fixed)
        return jnp.zeros((number_of,), jnp.int32).at[ranking[jnp.where(places < fixed, places, passed)]].set(jnp.asarray(lengths, jnp.int32))

    lengths = jnp.where(number % 4 == 0, named(crowded, number // 4), named(ordinary, number - number // 4 - 1))
    mixed = jax.random.permutation(jax.random.fold_in(own, 3), number_of)
    donor, receiver = mixed[0:number_of // 2 * 2:2], mixed[1:number_of // 2 * 2:2]
    slack = jnp.minimum(lengths[donor] - 1, bound - lengths[receiver]) // 2
    slack = jnp.where((donor == ranking[0]) | (receiver == ranking[0]) | (lengths[receiver] == 0), 0, jnp.maximum(slack, 0))
    passed = jax.random.randint(jax.random.fold_in(own, 4), (number_of // 2,), 0, 1 << 20) % (slack + 1)
    lengths = lengths.at[donor].add(-passed).at[receiver].add(passed)
    members = jnp.searchsorted(jnp.cumsum(lengths), jnp.arange(rows * top), side="right").astype(jnp.int32)
    table = members.reshape(top, rows).T
    table = table[jax.random.permutation(jax.random.fold_in(own, 1), rows)]
    rotation = jax.random.randint(jax.random.fold_in(own, 2), (rows, 1), 0, top)
    return jnp.take_along_axis(table, (jnp.arange(top)[None, :] + rotation) % top, axis=1)


def load_shares(count, total, most, skew, full):
    portions = [(1 << 20) // math.isqrt(rank ** skew) + 1 for rank in range(1, count + 1)]
    largest = most if full else min(most, max(-(-total // count), total * portions[0] // sum(portions)))
    least = 1 if total - largest >= count - 1 else 0
    given, rest = [largest] + [least] * (count - 1), total - largest - least * (count - 1)
    while rest > 0:
        free = [i for i in range(1, count) if given[i] < largest] or [i for i in range(1, count) if given[i] < most]
        mass, remaining = sum([portions[i] for i in free]), rest
        for i in free:
            extra = min(most - given[i], max(1, remaining * portions[i] // mass), rest)
            given[i] = given[i] + extra
            rest = rest - extra
    return np.array(given)


def gaussian(key, extent, spread, limit, shards=(), held_as=jnp.bfloat16):
    array = spread * jax.random.normal(key, extent, jnp.float32)
    if shards:
        array = array * block_scale(key, extent, shards, -0.22, 0.18)
    return jnp.clip(array, -limit, limit).astype(held_as)


def setup_inputs(seed: int = 0) -> dict:
    streams_of = jax.random.split(jax.random.key(seed), 9)
    queries = gaussian(streams_of[0], (NQ, D), 1.0, 6.0, ((0, 128),), jnp.float32)
    probes_keys = jax.random.split(jax.random.fold_in(streams_of[1], 1), NQ // Q_DEV)
    probes_turns = jax.random.permutation(jax.random.fold_in(streams_of[1], 3), NQ // Q_DEV)
    probes = jax.vmap(lambda own, number: assign_block(jax.random.fold_in(streams_of[1], 2), own, number, Q_DEV, LISTS, PROBE, MOST, 2))(probes_keys, probes_turns).reshape((NQ, PROBE))
    codes = draw_codes(jax.random.fold_in(streams_of[8], 71), 0)
    scale = jnp.clip(jnp.exp(math.log(0.00032) - 2.0794415 * jax.random.uniform(streams_of[3], (LISTS, D), jnp.float32) ** block_scale(streams_of[3], (LISTS, D), ((0, 128),), -0.2, 0.2)), 3.9999998989515007e-05, 0.00032)
    offset = gaussian(streams_of[4], (LISTS, D), 0.03125, 0.5, ((0, 128),), jnp.float32)
    tile_counts = ragged(streams_of[5], LISTS, LISTS * (TILES + 1) // 2, TILES, 2).astype(jnp.int32)
    raw_vectors = gaussian(streams_of[6], (VECS, D), 0.03125, 0.5, ((0, 128),), jnp.float32)
    candidates = draw_candidates(jax.random.fold_in(streams_of[8], 71), 0)
    return {"queries": queries, "probes": probes, "codes": codes, "scale": scale, "offset": offset, "tile_counts": tile_counts, "raw_vectors": raw_vectors, "candidates": candidates}


def reference(queries, probes, codes, scale, offset, tile_counts, raw_vectors, candidates):
    list_cap = min(N_GROUP * N_SLAB * MOST, NQ)
    row_ids = jnp.arange(ROWS, dtype=jnp.int32)

    def one_list(list_id):
        hit_mask = jnp.any(probes == list_id, axis=1)
        order_idx = jnp.argsort(jnp.where(hit_mask, 0, 1).astype(jnp.int32), stable=True).astype(jnp.int32)[:list_cap]
        chosen = queries[order_idx]
        folded = (chosen * scale[list_id]).astype(jnp.bfloat16)
        scores = jnp.dot(folded.astype(jnp.float32), codes[list_id].astype(jnp.float32).T, precision=lax.Precision.HIGHEST)
        row_valid = row_ids < tile_counts[list_id] * TILE
        best_score = jnp.max(jnp.where(row_valid[None, :], scores, -1e30), axis=1)
        base_score = jnp.dot(chosen, offset[list_id], precision=lax.Precision.HIGHEST)
        return jnp.zeros((NQ,), jnp.float32).at[order_idx].set(best_score + base_score)

    score_table = lax.map(one_list, jnp.arange(LISTS, dtype=jnp.int32))
    list_best = score_table[probes, jnp.arange(NQ, dtype=jnp.int32)[:, None]]

    def one_query(pair):
        query, vector_ids = pair
        return jnp.dot(raw_vectors[vector_ids], query, precision=lax.Precision.HIGHEST)

    rerank = lax.map(one_query, (queries, candidates))
    return list_best, rerank
```

```python
import functools

import jax
import jax.numpy as jnp
from jax import lax
from jax.experimental import pallas as pl
from jax.experimental.pallas import tpu as pltpu
from jax.sharding import PartitionSpec as P

TILE = 256
AXES = ("group", "slab")
ROWS = 40
F32 = jnp.float32
BF16 = jnp.bfloat16
HIGH = lax.Precision.HIGHEST
NT = (((1,), (1,)), ((), ()))
NN = (((1,), (0,)), ((), ()))


def dot(a, b, dims=NN, precision=None):
    return lax.dot_general(a, b, dims, precision=precision, preferred_element_type=F32)


def iota(shape, dim):
    return lax.broadcasted_iota(jnp.int32, shape, dim)


def vmem():
    return pl.BlockSpec(memory_space=pltpu.VMEM)


def smem():
    return pl.BlockSpec(memory_space=pltpu.SMEM)


def hbm():
    return pl.BlockSpec(memory_space=pl.ANY)


def pack_kernel(me_ref, q_ref, p_ref, c_ref, out_ref):
    q_dev = q_ref.shape[0]
    for q in range(q_dev):
        for c in range(8):
            out_ref[q * 8 + c : q * 8 + c + 1, :] = q_ref[q : q + 1, c * 128 : (c + 1) * 128]
    probes = p_ref[...].astype(F32)
    out_ref[32:33, :] = jnp.concatenate([probes[q : q + 1, :] for q in range(q_dev)], axis=1)
    cands = c_ref[...].astype(F32)
    out_ref[33:34, :] = jnp.concatenate([cands[0:1, :], cands[1:2, :]], axis=1)
    out_ref[34:35, :] = jnp.concatenate([cands[2:3, :], cands[3:4, :]], axis=1)
    out_ref[35:40, :] = jnp.full((5, 128), me_ref[0], jnp.int32).astype(F32)


def pack(me, queries, probes, candidates):
    return pl.pallas_call(
        pack_kernel,
        out_shape=jax.ShapeDtypeStruct((ROWS, 128), F32),
        in_specs=[smem(), vmem(), vmem(), vmem()],
        out_specs=vmem(),
    )(me, queries, probes, candidates)


def split_kernel(v_ref, hi_ref, lo_ref):
    v = v_ref[...]
    hi = v.astype(BF16)
    hi_ref[...] = hi
    lo_ref[...] = (v - hi.astype(F32)).astype(BF16)


def split(v):
    rows, width = v.shape
    blk = pl.BlockSpec((256, width), lambda i: (i, 0))
    return pl.pallas_call(
        split_kernel,
        grid=(rows // 256,),
        out_shape=[jax.ShapeDtypeStruct(v.shape, BF16)] * 2,
        in_specs=[blk],
        out_specs=[blk, blk],
    )(v)


def score_kernel(
    me_ref, tc_ref, *refs, n_blocks, per_block, n_lists, n_rows
):
    blocks = refs[:n_blocks]
    scale_ref, offset_ref, vhi_ref, vlo_ref, codes_ref, out_ref = refs[n_blocks : n_blocks + 6]
    code_buf, fold, base_acc, qhi, qlo, sems = refs[n_blocks + 6 :]
    me = me_ref[0]
    n_tiles = n_rows // TILE
    dev = n_blocks * per_block

    for l in range(n_lists):
        for t in range(n_tiles):
            pltpu.make_async_copy(
                codes_ref.at[l, pl.ds(t * TILE, TILE), :],
                code_buf.at[l, pl.ds(t * TILE, TILE), :],
                sems.at[l, t],
            ).start()

    def rows_of(r):
        return jnp.concatenate(
            [b[pl.ds(r, per_block, stride=ROWS), :] for b in blocks], axis=0
        )

    probe = rows_of(32)
    eq = jnp.concatenate(
        [(probe == (me * n_lists + l).astype(F32)).astype(BF16) for l in range(n_lists)], axis=0
    )
    seg = (iota((128, 512), 0) // 32 == iota((128, 512), 1) // 128).astype(BF16)
    hits = dot(eq, seg)
    ident = rows_of(35)
    perm = (ident == iota((dev, 128), 1).astype(F32)).astype(F32)

    for b in range(n_blocks):
        for g in range(per_block // 8):
            r0 = b * per_block + g * 8
            q_val = [
                [blocks[b][pl.ds(g * 8 * ROWS + q * 8 + c, 8, stride=ROWS), :] for c in range(8)]
                for q in range(4)
            ]
            for q in range(4):
                for c in range(8):
                    x = q_val[q][c]
                    hi = x.astype(BF16)
                    qhi[q * dev + r0 : q * dev + r0 + 8, c * 128 : (c + 1) * 128] = hi.astype(F32)
                    qlo[q * dev + r0 : q * dev + r0 + 8, c * 128 : (c + 1) * 128] = x - hi.astype(F32)
            for l in range(n_lists):
                h = [hits[l * dev + r0 : l * dev + r0 + 8, q * 128 : (q + 1) * 128] for q in range(3)]
                m0, m1, m2 = h[0] > 0.5, h[1] > 0.5, h[2] > 0.5
                s1 = (h[0] + h[1]) > 1.5
                s2 = (h[0] + h[1] + h[2]) > 1.5
                acc = [None, None]
                for c in range(8):
                    x = [q_val[q][c] for q in range(4)]
                    first = jnp.where(m0, x[0], jnp.where(m1, x[1], jnp.where(m2, x[2], x[3])))
                    second = jnp.where(s1, x[1], jnp.where(s2, x[2], x[3]))
                    sc = scale_ref[l : l + 1, c * 128 : (c + 1) * 128]
                    of = offset_ref[l : l + 1, c * 128 : (c + 1) * 128]
                    for s, pick in enumerate((first, second)):
                        fold[l, s * dev + r0 : s * dev + r0 + 8, c * 128 : (c + 1) * 128] = pick * sc
                        part = pick * of
                        acc[s] = part if acc[s] is None else acc[s] + part
                for s in range(2):
                    base_acc[l, s * dev + r0 : s * dev + r0 + 8, :] = acc[s]

    ones = jnp.ones((8, 128), F32)
    out_rows = []
    for l in range(n_lists):
        folded = fold[l].astype(BF16)
        best = None
        for t in range(n_tiles):
            pltpu.make_async_copy(
                codes_ref.at[l, pl.ds(t * TILE, TILE), :],
                code_buf.at[l, pl.ds(t * TILE, TILE), :],
                sems.at[l, t],
            ).wait()
            s = dot(code_buf[l, t * TILE : (t + 1) * TILE, :], folded, NT)
            m = jnp.max(s.reshape(TILE // 8, 8, 2 * dev), axis=0)
            if t == 0:
                best = m
            else:
                best = jnp.where(t < tc_ref[l], jnp.maximum(best, m), best)
        best = jnp.max(best, axis=0, keepdims=True)
        base = dot(ones, base_acc[l], NT, HIGH)[0:1, :]
        total = best + base
        out_rows += [total[:, :dev], total[:, dev:]]

    cand = jnp.concatenate([rows_of(33), rows_of(34)], axis=1)
    v_dev = vhi_ref.shape[0]
    local_id = cand - (me * v_dev).astype(F32)
    mine = (local_id >= 0.0) & (local_id < float(v_dev))
    tri = (iota((256, 256), 0) < iota((256, 256), 1)).astype(BF16)
    rank = dot(mine.astype(BF16), tri)
    place = local_id + (iota((dev, 256), 1) // 64 * v_dev).astype(F32)
    wide = jnp.ones((256, 128), F32)
    spot = [
        dot(jnp.where(mine & (rank == float(s)), place, 0.0), wide, NN, HIGH) for s in range(4)
    ]
    spot = [(x + 0.5).astype(jnp.int32) for x in spot]
    found = [jnp.zeros((dev, 128), F32) for _ in range(4)]
    for q in range(4):
        hi = qhi[q * dev : (q + 1) * dev, :].astype(BF16)
        lo = qlo[q * dev : (q + 1) * dev, :].astype(BF16)
        for n in range(v_dev // 256):
            vh = vhi_ref[n * 256 : (n + 1) * 256, :]
            vl = vlo_ref[n * 256 : (n + 1) * 256, :]
            s = dot(hi, vh, NT) + dot(lo, vh, NT) + dot(hi, vl, NT)
            for h in range(2):
                lane = iota((dev, 128), 1) + (q * v_dev + n * 256 + h * 128)
                for k in range(4):
                    found[k] = jnp.where(spot[k] == lane, s[:, h * 128 : (h + 1) * 128], found[k])
    for k in range(4):
        out_rows.append(dot(ones, found[k], NT, HIGH)[0:1, :])
    pad = jnp.zeros((16 - len(out_rows), dev), F32)
    table = jnp.concatenate(out_rows + [pad], axis=0)
    table = dot(table, perm, NN, HIGH)
    table = jnp.concatenate([table, jnp.zeros((112, 128), F32)], axis=0)
    out_ref[...] = table.T


def score(me, tile_counts, blocks, scale, offset, vhi, vlo, codes):
    n_lists, n_rows, width = codes.shape
    per_block = blocks[0].shape[0]
    blocks = [b.reshape(per_block * ROWS, 128) for b in blocks]
    dev = per_block * len(blocks)
    return pl.pallas_call(
        functools.partial(
            score_kernel, n_blocks=len(blocks), per_block=per_block, n_lists=n_lists, n_rows=n_rows
        ),
        out_shape=jax.ShapeDtypeStruct((dev, 128), F32),
        in_specs=[smem(), smem()] + [vmem()] * (len(blocks) + 4) + [hbm()],
        out_specs=vmem(),
        scratch_shapes=[
            pltpu.VMEM(codes.shape, BF16),
            pltpu.VMEM((n_lists, 2 * dev, width), F32),
            pltpu.VMEM((n_lists, 2 * dev, 128), F32),
            pltpu.VMEM((4 * dev, width), F32),
            pltpu.VMEM((4 * dev, width), F32),
            pltpu.SemaphoreType.DMA((n_lists, n_rows // TILE)),
        ],
        compiler_params=pltpu.CompilerParams(vmem_limit_bytes=56 * 1024 * 1024),
    )(me, tile_counts, *blocks, scale, offset, vhi, vlo, codes)


def pick_kernel(got_ref, p_ref, c_ref, best_ref, rerank_ref):
    got = got_ref[...].T[0:16, :]
    probes, cands = p_ref[...], c_ref[...]
    name = jnp.concatenate([probes[q : q + 1, :] for q in range(4)], axis=1)
    across = jnp.broadcast_to(name, (128, 128))
    down = across.T
    earlier = iota((128, 128), 0) // 32 < iota((128, 128), 1) // 32
    rank = jnp.sum(jnp.where((down == across) & earlier, 1, 0), axis=0, keepdims=True)
    row_of = (name % 4) * 2 + rank
    pairs = [(name // 4, row_of)]
    ids = [
        jnp.concatenate([cands[0:1, :], cands[1:2, :]], axis=1),
        jnp.concatenate([cands[2:3, :], cands[3:4, :]], axis=1),
    ]
    owner = [x // 1024 for x in ids]
    wide = [jnp.broadcast_to(x, (128, 128)) for x in owner]
    tall = [x.T for x in wide]
    before = iota((128, 128), 0) < iota((128, 128), 1)
    first = jnp.sum(jnp.where((tall[0] == wide[0]) & before, 1, 0), axis=0, keepdims=True)
    second = jnp.sum(jnp.where(tall[0] == wide[1], 1, 0), axis=0, keepdims=True) + jnp.sum(
        jnp.where((tall[1] == wide[1]) & before, 1, 0), axis=0, keepdims=True
    )
    pairs += [(owner[0], 8 + first), (owner[1], 8 + second)]
    vals = []
    for holder, row in pairs:
        hot = (iota((128, 128), 0) == holder).astype(F32)
        w = dot(got, hot, NN, HIGH)
        vals.append(jnp.sum(jnp.where(iota((16, 128), 0) == row, w, 0.0), axis=0, keepdims=True))
    best_ref[...] = jnp.concatenate([vals[0][:, q * 32 : (q + 1) * 32] for q in range(4)], axis=0)
    rerank_ref[...] = jnp.concatenate(
        [vals[1 + q // 2][:, (q % 2) * 64 : (q % 2) * 64 + 64] for q in range(4)], axis=0
    )


def pick(got, probes, candidates):
    return pl.pallas_call(
        pick_kernel,
        out_shape=(
            jax.ShapeDtypeStruct(probes.shape, F32),
            jax.ShapeDtypeStruct(candidates.shape, F32),
        ),
        in_specs=[vmem()] * 3,
        out_specs=(vmem(), vmem()),
    )(got, probes, candidates)


def place_of(x, z, y, c):
    return ((x * 4 + z) * 4 + y) * 2 + c


def shift_pairs(step, axis_of_core):
    pairs = []
    for x in range(4):
        for z in range(4):
            for y in range(4):
                for c in range(2):
                    at = {"x": x, "z": z, "y": y}
                    at[axis_of_core[c]] = (at[axis_of_core[c]] + step) % 4
                    pairs.append((place_of(x, z, y, c), place_of(at["x"], at["z"], at["y"], c)))
    return pairs


def other_core():
    return [(i, i ^ 1) for i in range(128)]


ORDERS = ("xy", "yz", "zx")


def local(queries, probes, codes, scale, offset, tile_counts, raw_vectors, candidates):
    me = lax.axis_index(AXES).astype(jnp.int32).reshape(1)
    packet = pack(me, queries, probes, candidates)
    vhi, vlo = split(raw_vectors)
    have = packet[None]
    for stage in range(2):
        got = [lax.ppermute(have, AXES, shift_pairs(k, ORDERS[stage])) for k in (1, 2, 3)]
        have = jnp.concatenate([have] + got, axis=0)
    blocks = [have] + [lax.ppermute(have, AXES, shift_pairs(k, ORDERS[2])) for k in (1, 3, 2)]
    blocks = blocks + [lax.ppermute(b, AXES, other_core()) for b in blocks]
    found = score(me, tile_counts, blocks, scale, offset, vhi, vlo, codes)
    devices = found.shape[0]
    back = lax.all_to_all(found.reshape(devices, 1, 128), AXES, split_axis=0, concat_axis=0, tiled=True)
    return pick(back.reshape(devices, 128), probes, candidates)


def solution(mesh):
    in_specs = (
        P(AXES, None),
        P(AXES, None),
        P(AXES, None, None),
        P(AXES, None),
        P(AXES, None),
        P(AXES),
        P(AXES, None),
        P(AXES, None),
    )
    out_specs = (P(AXES, None), P(AXES, None))
    return jax.shard_map(local, mesh=mesh, in_specs=in_specs, out_specs=out_specs, check_vma=False)
```

```python
import functools

import jax
import jax.numpy as jnp
from jax import lax
from jax.experimental import pallas as pl
from jax.experimental.pallas import tpu as pltpu
from jax.sharding import Mesh, PartitionSpec as P

TILE = 256
AXIS = "device"
VLIM = 40
ROWS = 40
F32 = jnp.float32
BF16 = jnp.bfloat16
HIGH = lax.Precision.HIGHEST
NT = (((1,), (1,)), ((), ()))
NN = (((1,), (0,)), ((), ()))


def dot(a, b, dims=NN, precision=None):
    return lax.dot_general(a, b, dims, precision=precision, preferred_element_type=F32)


def iota(shape, dim):
    return lax.broadcasted_iota(jnp.int32, shape, dim)


def vmem():
    return pl.BlockSpec(memory_space=pltpu.VMEM)


def smem():
    return pl.BlockSpec(memory_space=pltpu.SMEM)


def in_hbm(x):
    return pltpu.with_memory_space_constraint(x, pltpu.HBM)


def hbm():
    return pl.BlockSpec(memory_space=pl.ANY)


def pack_kernel(me_ref, q_hbm, p_hbm, c_hbm, out_ref, q_ref, p_ref, c_ref, sems):
    pairs = [(q_hbm, q_ref), (p_hbm, p_ref), (c_hbm, c_ref)]
    arrivals = [pltpu.make_async_copy(src, dst, sems.at[i]) for i, (src, dst) in enumerate(pairs)]
    for copy in arrivals:
        copy.start()
    for copy in arrivals:
        copy.wait()
    q_dev = q_ref.shape[0]
    queries = q_ref[...]
    rows = [queries[q : q + 1, c * 128 : (c + 1) * 128] for q in range(q_dev) for c in range(8)]
    probes = p_ref[...].astype(F32)
    rows.append(jnp.concatenate([probes[q : q + 1, :] for q in range(q_dev)], axis=1))
    cands = c_ref[...].astype(F32)
    rows.append(jnp.concatenate([cands[0:1, :], cands[1:2, :]], axis=1))
    rows.append(jnp.concatenate([cands[2:3, :], cands[3:4, :]], axis=1))
    rows.append(jnp.full((ROWS - len(rows), 128), me_ref[0], jnp.int32).astype(F32))
    packet = jnp.concatenate(rows, axis=0)
    for i in range(out_ref.shape[0]):
        out_ref[i] = packet


def pack(me, queries, probes, candidates, copies):
    return pl.pallas_call(
        pack_kernel,
        out_shape=jax.ShapeDtypeStruct((copies, ROWS, 128), F32),
        in_specs=[smem()] + [hbm()] * 3,
        out_specs=vmem(),
        scratch_shapes=[pltpu.VMEM(x.shape, x.dtype) for x in (queries, probes, candidates)]
        + [pltpu.SemaphoreType.DMA((3,))],
        compiler_params=pltpu.CompilerParams(vmem_limit_bytes=8 * 1024 * 1024),
    )(me, *[in_hbm(x) for x in (queries, probes, candidates)])


def score_kernel(me_ref, *refs, n_blocks, n_lists, n_rows, v_dev):
    blocks = refs[:n_blocks]
    tiles_hbm, scale_hbm, offset_hbm, vecs_hbm, codes_hbm, out_ref = refs[n_blocks : n_blocks + 6]
    (
        tiles_ref, scale_ref, offset_ref, codes_ref, vecs_ref,
        fold, base_acc, prod, spot_v, spot_s, sem, small_sems, vec_sems, code_sems,
    ) = refs[n_blocks + 6 :]
    me = me_ref[0]
    code_copies = [
        pltpu.make_async_copy(codes_hbm.at[l], codes_ref.at[l], code_sems.at[l])
        for l in range(n_lists)
    ]
    vec_copies = [
        pltpu.make_async_copy(
            vecs_hbm.at[:, pl.ds(c * 128, 128)], vecs_ref.at[:, c, :], vec_sems.at[c]
        )
        for c in range(8)
    ]
    small_copies = [
        pltpu.make_async_copy(src, dst, small_sems.at[i])
        for i, (src, dst) in enumerate(
            [(scale_hbm, scale_ref), (offset_hbm, offset_ref), (tiles_hbm, tiles_ref)]
        )
    ]
    for copy in small_copies + [code_copies[0]] + vec_copies + code_copies[1:]:
        copy.start()
    n_tiles = n_rows // TILE
    per = blocks[0].shape[0] // ROWS
    dev = n_blocks * per

    def rows_of(r):
        return jnp.concatenate([b[pl.ds(r, per, stride=ROWS), :] for b in blocks], axis=0)

    cand = jnp.concatenate([rows_of(33), rows_of(34)], axis=1).astype(jnp.int32)
    local_id = cand - me * v_dev
    mine = (local_id >= 0) & (local_id < v_dev)
    tri = (iota((256, 256), 0) < iota((256, 256), 1)).astype(BF16)
    rank = dot(mine.astype(BF16), tri)
    place = local_id + iota((dev, 256), 1) // 64 * v_dev
    high = (place // 64).astype(F32)
    low = (place % 64).astype(F32)
    one = jnp.ones((8, 256), BF16)
    spots = []
    for k in range(4):
        here = mine & (rank == float(k))
        hi = dot(one, jnp.where(here, high, 0.0).astype(BF16), NT)
        lo = dot(one, jnp.where(here, low, 0.0).astype(BF16), NT)
        spots.append((hi[0:1, :] * 64.0 + lo[0:1, :]).astype(jnp.int32))
    spot_v[...] = jnp.concatenate(spots + spots, axis=0)
    to_smem = pltpu.make_async_copy(spot_v, spot_s, sem)
    to_smem.start()

    probe = rows_of(32)
    eq = jnp.concatenate(
        [(probe == (me * n_lists + l).astype(F32)).astype(BF16) for l in range(n_lists)], axis=0
    )
    seg = (iota((128, 384), 0) // 32 == iota((128, 384), 1) // 128).astype(BF16)
    hits = dot(eq, seg)
    ident = rows_of(35)
    perm = (ident == iota((dev, 128), 1).astype(F32)).astype(F32)

    for copy in small_copies:
        copy.wait()
    for b in range(n_blocks):
        r0 = b * per
        for l in range(n_lists):
            h = [hits[l * dev + r0 : l * dev + r0 + per, q * 128 : (q + 1) * 128] for q in range(3)]
            m0, m1, m2 = h[0] > 0.5, h[1] > 0.5, h[2] > 0.5
            s1 = (h[0] + h[1]) > 1.5
            s2 = (h[0] + h[1] + h[2]) > 1.5
            acc = [None, None]
            for c in range(8):
                x = [blocks[b][pl.ds(q * 8 + c, per, stride=ROWS), :] for q in range(4)]
                first = jnp.where(m0, x[0], jnp.where(m1, x[1], jnp.where(m2, x[2], x[3])))
                second = jnp.where(s1, x[1], jnp.where(s2, x[2], x[3]))
                sc = scale_ref[l : l + 1, c * 128 : (c + 1) * 128]
                of = offset_ref[l : l + 1, c * 128 : (c + 1) * 128]
                for s, take in enumerate((first, second)):
                    fold[l, s * dev + r0 : s * dev + r0 + per, c * 128 : (c + 1) * 128] = (
                        take * sc
                    ).astype(BF16)
                    part = take * of
                    acc[s] = part if acc[s] is None else acc[s] + part
            for s in range(2):
                base_acc[l, s * dev + r0 : s * dev + r0 + per, :] = acc[s]

    to_smem.wait()
    for copy in vec_copies:
        copy.wait()

    def gather(b):
        for i in range(per):
            for k in range(4):
                at = spot_s[k, b * per + i]
                q = pl.multiple_of(i * ROWS + at // v_dev * 8, 8)
                j = (k * dev + b * per + i) * 8
                prod[j : j + 8, :] = vecs_ref[at % v_dev] * blocks[b][pl.ds(q, 8), :]

    out_rows = []
    steps = n_lists * n_tiles
    done = 0
    for l in range(n_lists):
        folded = fold[l]
        code_copies[l].wait()
        best = None
        for t in range(n_tiles):
            s = dot(codes_ref[l, t * TILE : (t + 1) * TILE, :], folded, NT)
            m = jnp.max(s.reshape(TILE // 8, 8, 2 * dev), axis=0)
            if t == 0:
                best = m
            else:
                best = jnp.where(t < tiles_ref[l], jnp.maximum(best, m), best)
            if (l * n_tiles + t + 1) * n_blocks // steps > done:
                gather(done)
                done += 1
        best = jnp.max(best, axis=0, keepdims=True)
        for s in range(2):
            base = base_acc[l, s * dev : (s + 1) * dev, :].T
            out_rows.append(best[:, s * dev : (s + 1) * dev] + jnp.sum(base, axis=0, keepdims=True))
    for k in range(4):
        total = None
        for c in range(8):
            x = prod[pl.ds(k * dev * 8 + c, dev, stride=8), :]
            total = x if total is None else total + x
        out_rows.append(jnp.sum(total.T, axis=0, keepdims=True))
    pad = jnp.zeros((16 - len(out_rows), dev), F32)
    table = jnp.concatenate(out_rows + [pad], axis=0)
    table = dot(table, perm, NN, HIGH)
    table = jnp.concatenate([table, jnp.zeros((112, 128), F32)], axis=0)
    out_ref[...] = table.T


def score(me, tile_counts, blocks, scale, offset, vectors, codes):
    n_lists, n_rows, width = codes.shape
    v_dev = vectors.shape[0]
    per = blocks[0].shape[0]
    blocks = [b.reshape(per * ROWS, 128) for b in blocks]
    dev = per * len(blocks)
    body = functools.partial(
        score_kernel, n_blocks=len(blocks), n_lists=n_lists, n_rows=n_rows, v_dev=v_dev
    )
    return pl.pallas_call(
        body,
        out_shape=jax.ShapeDtypeStruct((dev, 128), F32),
        in_specs=[smem()] + [vmem()] * len(blocks) + [hbm()] * 5,
        out_specs=vmem(),
        scratch_shapes=[
            pltpu.SMEM(tile_counts.shape, jnp.int32),
            pltpu.VMEM(scale.shape, F32),
            pltpu.VMEM(offset.shape, F32),
            pltpu.VMEM(codes.shape, BF16),
            pltpu.VMEM((v_dev, 8, 128), F32),
            pltpu.VMEM((n_lists, 2 * dev, width), BF16),
            pltpu.VMEM((n_lists, 2 * dev, 128), F32),
            pltpu.VMEM((4 * dev * 8, 128), F32),
            pltpu.VMEM((8, dev), jnp.int32),
            pltpu.SMEM((8, dev), jnp.int32),
            pltpu.SemaphoreType.DMA,
            pltpu.SemaphoreType.DMA((3,)),
            pltpu.SemaphoreType.DMA((8,)),
            pltpu.SemaphoreType.DMA((n_lists,)),
        ],
        compiler_params=pltpu.CompilerParams(vmem_limit_bytes=VLIM * 1024 * 1024),
    )(
        me, *blocks, *[in_hbm(x) for x in (tile_counts, scale, offset, vectors, codes)]
    )


def pick_kernel(got_ref, p_ref, c_ref, best_ref, rerank_ref):
    got = got_ref[...].T[0:16, :]
    probes, cands = p_ref[...], c_ref[...]
    name = jnp.concatenate([probes[q : q + 1, :] for q in range(4)], axis=1)
    across = jnp.broadcast_to(name, (128, 128))
    down = across.T
    earlier = iota((128, 128), 0) // 32 < iota((128, 128), 1) // 32
    rank = jnp.sum(jnp.where((down == across) & earlier, 1, 0), axis=0, keepdims=True)
    row_of = (name % 4) * 2 + rank
    pairs = [(name // 4, row_of)]
    ids = [
        jnp.concatenate([cands[0:1, :], cands[1:2, :]], axis=1),
        jnp.concatenate([cands[2:3, :], cands[3:4, :]], axis=1),
    ]
    owner = [x // 1024 for x in ids]
    wide = [jnp.broadcast_to(x, (128, 128)) for x in owner]
    tall = [x.T for x in wide]
    before = iota((128, 128), 0) < iota((128, 128), 1)
    first = jnp.sum(jnp.where((tall[0] == wide[0]) & before, 1, 0), axis=0, keepdims=True)
    second = jnp.sum(jnp.where(tall[0] == wide[1], 1, 0), axis=0, keepdims=True) + jnp.sum(
        jnp.where((tall[1] == wide[1]) & before, 1, 0), axis=0, keepdims=True
    )
    pairs += [(owner[0], 8 + first), (owner[1], 8 + second)]
    vals = []
    for holder, row in pairs:
        hot = (iota((128, 128), 0) == holder).astype(F32)
        w = dot(got, hot, NN, HIGH)
        vals.append(jnp.sum(jnp.where(iota((16, 128), 0) == row, w, 0.0), axis=0, keepdims=True))
    best_ref[...] = jnp.concatenate([vals[0][:, q * 32 : (q + 1) * 32] for q in range(4)], axis=0)
    rerank_ref[...] = jnp.concatenate(
        [vals[1 + q // 2][:, (q % 2) * 64 : (q % 2) * 64 + 64] for q in range(4)], axis=0
    )


def pick(got, probes, candidates):
    return pl.pallas_call(
        pick_kernel,
        out_shape=(
            jax.ShapeDtypeStruct(probes.shape, F32),
            jax.ShapeDtypeStruct(candidates.shape, F32),
        ),
        in_specs=[vmem()] * 3,
        out_specs=(vmem(), vmem()),
        compiler_params=pltpu.CompilerParams(vmem_limit_bytes=8 * 1024 * 1024),
    )(got, probes, candidates)


def place_of(at, core):
    return ((at["x"] * 4 + at["z"]) * 4 + at["y"]) * 2 + core


def chips():
    return [{"x": x, "z": z, "y": y} for x in range(4) for z in range(4) for y in range(4)]


def plane_groups(last):
    return [
        [place_of(at, core) for at in chips() if at[last[core]] == place]
        for core in range(2)
        for place in range(4)
    ]


def shift_pairs(step, last):
    pairs = []
    for at in chips():
        for core in range(2):
            to = dict(at)
            to[last[core]] = (at[last[core]] + step) % 4
            pairs.append((place_of(at, core), place_of(to, core)))
    return pairs


def other_core():
    return [(i, i ^ 1) for i in range(128)]


LAST = "zy"


def local(queries, probes, codes, scale, offset, tile_counts, raw_vectors, candidates):
    me = lax.axis_index(AXIS).astype(jnp.int32).reshape(1)
    copies = pack(me, queries, probes, candidates, 16)
    have = lax.all_to_all(
        copies, AXIS, split_axis=0, concat_axis=0, tiled=True, axis_index_groups=plane_groups(LAST)
    )
    blocks = [have] + [lax.ppermute(have, AXIS, shift_pairs(k, LAST)) for k in (1, 3, 2)]
    blocks = blocks + [lax.ppermute(b, AXIS, other_core()) for b in blocks]
    found = score(me, tile_counts, blocks, scale, offset, raw_vectors, codes)
    devices = found.shape[0]
    back = lax.all_to_all(found.reshape(devices, 1, 128), AXIS, split_axis=0, concat_axis=0, tiled=True)
    return pick(back.reshape(devices, 128), probes, candidates)


def solution(mesh):
    flat = Mesh(mesh.devices.reshape(-1), (AXIS,))
    in_specs = (
        P(AXIS, None),
        P(AXIS, None),
        P(AXIS, None, None),
        P(AXIS, None),
        P(AXIS, None),
        P(AXIS),
        P(AXIS, None),
        P(AXIS, None),
    )
    out_specs = (P(AXIS, None), P(AXIS, None))
    return jax.shard_map(local, mesh=flat, in_specs=in_specs, out_specs=out_specs, check_vma=False)
```

```python
import functools

import jax
import jax.numpy as jnp
from jax import lax
from jax.experimental import pallas as pl
from jax.experimental.pallas import tpu as pltpu
from jax.sharding import Mesh, PartitionSpec as P

TILE = 256
AXIS = "device"
VLIM = 28
ROWS = 40
F32 = jnp.float32
BF16 = jnp.bfloat16
HIGH = lax.Precision.HIGHEST
NT = (((1,), (1,)), ((), ()))
NN = (((1,), (0,)), ((), ()))


def dot(a, b, dims=NN, precision=None):
    return lax.dot_general(a, b, dims, precision=precision, preferred_element_type=F32)


def iota(shape, dim):
    return lax.broadcasted_iota(jnp.int32, shape, dim)


def choose(values, hot):
    high = values.astype(BF16)
    rest = values - high.astype(F32)
    mid = rest.astype(BF16)
    low = (rest - mid.astype(F32)).astype(BF16)
    n = values.shape[0]
    out = dot(jnp.concatenate([high, mid, low], axis=0), hot)
    return out[:n] + out[n : 2 * n] + out[2 * n :]


def vmem():
    return pl.BlockSpec(memory_space=pltpu.VMEM)


def smem():
    return pl.BlockSpec(memory_space=pltpu.SMEM)


def in_hbm(x):
    return pltpu.with_memory_space_constraint(x, pltpu.HBM)


def hbm():
    return pl.BlockSpec(memory_space=pl.ANY)


def pack_kernel(me_ref, q_hbm, p_hbm, c_hbm, out_ref, q_ref, p_ref, c_ref, sems):
    pairs = [(q_hbm, q_ref), (p_hbm, p_ref), (c_hbm, c_ref)]
    arrivals = [pltpu.make_async_copy(src, dst, sems.at[i]) for i, (src, dst) in enumerate(pairs)]
    for copy in arrivals:
        copy.start()
    for copy in arrivals:
        copy.wait()
    q_dev = q_ref.shape[0]
    queries = q_ref[...]
    rows = [queries[q : q + 1, c * 128 : (c + 1) * 128] for q in range(q_dev) for c in range(8)]
    probes = p_ref[...].astype(F32)
    rows.append(jnp.concatenate([probes[q : q + 1, :] for q in range(q_dev)], axis=1))
    cands = c_ref[...].astype(F32)
    rows.append(jnp.concatenate([cands[0:1, :], cands[1:2, :]], axis=1))
    rows.append(jnp.concatenate([cands[2:3, :], cands[3:4, :]], axis=1))
    rows.append(jnp.full((ROWS - len(rows), 128), me_ref[0], jnp.int32).astype(F32))
    packet = jnp.concatenate(rows, axis=0)
    for i in range(out_ref.shape[0]):
        out_ref[i] = packet


def pack(me, queries, probes, candidates, copies):
    return pl.pallas_call(
        pack_kernel,
        out_shape=jax.ShapeDtypeStruct((copies, ROWS, 128), F32),
        in_specs=[smem()] + [hbm()] * 3,
        out_specs=vmem(),
        scratch_shapes=[pltpu.VMEM(x.shape, x.dtype) for x in (queries, probes, candidates)]
        + [pltpu.SemaphoreType.DMA((3,))],
        compiler_params=pltpu.CompilerParams(vmem_limit_bytes=8 * 1024 * 1024),
    )(me, *[in_hbm(x) for x in (queries, probes, candidates)])


def fetch_kernel(have_ref, vecs_ref, have_out, vecs_out, sems):
    copies = [
        pltpu.make_async_copy(
            vecs_ref.at[:, pl.ds(c * 128, 128)], vecs_out.at[:, c, :], sems.at[c]
        )
        for c in range(8)
    ]
    for copy in copies:
        copy.start()
    have_out[...] = have_ref[...]
    for copy in copies:
        copy.wait()


def fetch(have, vectors):
    return pl.pallas_call(
        fetch_kernel,
        out_shape=(
            jax.ShapeDtypeStruct(have.shape, F32),
            pltpu.VMEM((vectors.shape[0], 8, 128), F32),
        ),
        in_specs=[vmem(), hbm()],
        out_specs=(vmem(), vmem()),
        scratch_shapes=[pltpu.SemaphoreType.DMA((8,))],
        compiler_params=pltpu.CompilerParams(vmem_limit_bytes=2 * 1024 * 1024),
        cost_estimate=pl.CostEstimate(
            flops=0, transcendentals=0, bytes_accessed=2 * vectors.size * 4
        ),
    )(have, in_hbm(vectors))


def score_kernel(me_ref, *refs, n_blocks, n_lists, n_rows, v_dev):
    blocks = refs[:n_blocks]
    tiles_hbm, scale_hbm, offset_hbm, vecs_ref, codes_hbm, out_ref = refs[n_blocks : n_blocks + 6]
    (
        tiles_ref, scale_ref, offset_ref, codes_ref,
        fold, base_acc, prod, spot_v, spot_s, sem, small_sems, code_sems,
    ) = refs[n_blocks + 6 :]
    me = me_ref[0]
    code_copies = [
        pltpu.make_async_copy(codes_hbm.at[l], codes_ref.at[l], code_sems.at[l])
        for l in range(n_lists)
    ]
    small_copies = [
        pltpu.make_async_copy(src, dst, small_sems.at[i])
        for i, (src, dst) in enumerate(
            [(scale_hbm, scale_ref), (offset_hbm, offset_ref), (tiles_hbm, tiles_ref)]
        )
    ]
    for copy in small_copies + code_copies[:1]:
        copy.start()
    n_tiles = n_rows // TILE
    per = blocks[0].shape[0] // ROWS
    dev = n_blocks * per

    def rows_of(r):
        return jnp.concatenate([b[pl.ds(r, per, stride=ROWS), :] for b in blocks], axis=0)

    cand = jnp.concatenate([rows_of(33), rows_of(34)], axis=1).astype(jnp.int32)
    local_id = cand - me * v_dev
    mine = (local_id >= 0) & (local_id < v_dev)
    tri = (iota((256, 256), 0) < iota((256, 256), 1)).astype(BF16)
    rank = dot(mine.astype(BF16), tri)
    place = local_id + iota((dev, 256), 1) // 64 * v_dev
    high = (place // 64).astype(F32)
    low = (place % 64).astype(F32)
    one = jnp.ones((8, 256), BF16)
    spots = []
    for k in range(4):
        here = mine & (rank == float(k))
        hi = dot(one, jnp.where(here, high, 0.0).astype(BF16), NT)
        lo = dot(one, jnp.where(here, low, 0.0).astype(BF16), NT)
        spots.append((hi[0:1, :] * 64.0 + lo[0:1, :]).astype(jnp.int32))
    first_row = iota((1, dev), 1) % per * ROWS
    spot_v[...] = jnp.concatenate(
        [x % v_dev for x in spots] + [x // v_dev * 8 + first_row for x in spots], axis=0
    )
    to_smem = pltpu.make_async_copy(spot_v, spot_s, sem)
    to_smem.start()

    probe = rows_of(32)
    eq = jnp.concatenate(
        [(probe == (me * n_lists + l).astype(F32)).astype(BF16) for l in range(n_lists)], axis=0
    )
    seg = (iota((128, 384), 0) // 32 == iota((128, 384), 1) // 128).astype(BF16)
    hits = dot(eq, seg)
    ident = rows_of(35)
    perm = (ident == iota((dev, 128), 1).astype(F32)).astype(BF16)

    for copy in small_copies:
        copy.wait()
    code_copies[1].start()
    for b in range(n_blocks):
        r0 = b * per
        if b == 4:
            code_copies[2].start()
        for l in range(n_lists):
            h = [hits[l * dev + r0 : l * dev + r0 + per, q * 128 : (q + 1) * 128] for q in range(3)]
            m0, m1, m2 = h[0] > 0.5, h[1] > 0.5, h[2] > 0.5
            s1 = (h[0] + h[1]) > 1.5
            s2 = (h[0] + h[1] + h[2]) > 1.5
            acc = [None, None]
            for c in range(8):
                x = [blocks[b][pl.ds(q * 8 + c, per, stride=ROWS), :] for q in range(4)]
                first = jnp.where(m0, x[0], jnp.where(m1, x[1], jnp.where(m2, x[2], x[3])))
                second = jnp.where(s1, x[1], jnp.where(s2, x[2], x[3]))
                sc = scale_ref[l : l + 1, c * 128 : (c + 1) * 128]
                of = offset_ref[l : l + 1, c * 128 : (c + 1) * 128]
                for s, take in enumerate((first, second)):
                    fold[l, s * dev + r0 : s * dev + r0 + per, c * 128 : (c + 1) * 128] = (
                        take * sc
                    ).astype(BF16)
                    part = take * of
                    acc[s] = part if acc[s] is None else acc[s] + part
            for s in range(2):
                base_acc[l, s * dev + r0 : s * dev + r0 + per, :] = acc[s]

    to_smem.wait()
    code_copies[3].start()

    def gather(part):
        for j in range(part * 4, part * 4 + 4):
            b = j // per
            for k in range(4):
                row, q = spot_s[k, j], pl.multiple_of(spot_s[4 + k, j], 8)
                to = (k * dev + j) * 8
                prod[to : to + 8, :] = vecs_ref[row] * blocks[b][pl.ds(q, 8), :]

    out_rows = []
    steps = n_lists * n_tiles
    done = 0
    for l in range(n_lists):
        folded = fold[l]
        code_copies[l].wait()
        best = None
        for t in range(n_tiles):
            s = dot(codes_ref[l, t * TILE : (t + 1) * TILE, :], folded, NT)
            m = jnp.max(s.reshape(TILE // 8, 8, 2 * dev), axis=0)
            if t == 0:
                best = m
            else:
                best = jnp.where(t < tiles_ref[l], jnp.maximum(best, m), best)
            if (l * n_tiles + t + 1) * (dev // 4) // steps > done:
                gather(done)
                done += 1
        best = jnp.max(best, axis=0, keepdims=True)
        for s in range(2):
            base = base_acc[l, s * dev : (s + 1) * dev, :].T
            out_rows.append(best[:, s * dev : (s + 1) * dev] + jnp.sum(base, axis=0, keepdims=True))
    for k in range(4):
        total = None
        for c in range(8):
            x = prod[pl.ds(k * dev * 8 + c, dev, stride=8), :]
            total = x if total is None else total + x
        out_rows.append(jnp.sum(total.T, axis=0, keepdims=True))
    pad = jnp.zeros((16 - len(out_rows), dev), F32)
    table = jnp.concatenate(out_rows + [pad], axis=0)
    table = choose(table, perm)
    table = jnp.concatenate([table, jnp.zeros((112, 128), F32)], axis=0)
    out_ref[...] = table.T


def score(me, tile_counts, blocks, scale, offset, vectors, codes):
    n_lists, n_rows, width = codes.shape
    v_dev = vectors.shape[0]
    per = blocks[0].shape[0]
    blocks = [b.reshape(per * ROWS, 128) for b in blocks]
    dev = per * len(blocks)
    body = functools.partial(
        score_kernel, n_blocks=len(blocks), n_lists=n_lists, n_rows=n_rows, v_dev=v_dev
    )
    return pl.pallas_call(
        body,
        out_shape=jax.ShapeDtypeStruct((dev, 128), F32),
        in_specs=[smem()] + [vmem()] * len(blocks) + [hbm()] * 3 + [vmem(), hbm()],
        out_specs=vmem(),
        scratch_shapes=[
            pltpu.SMEM(tile_counts.shape, jnp.int32),
            pltpu.VMEM(scale.shape, F32),
            pltpu.VMEM(offset.shape, F32),
            pltpu.VMEM(codes.shape, BF16),
            pltpu.VMEM((n_lists, 2 * dev, width), BF16),
            pltpu.VMEM((n_lists, 2 * dev, 128), F32),
            pltpu.VMEM((4 * dev * 8, 128), F32),
            pltpu.VMEM((8, dev), jnp.int32),
            pltpu.SMEM((8, dev), jnp.int32),
            pltpu.SemaphoreType.DMA,
            pltpu.SemaphoreType.DMA((3,)),
            pltpu.SemaphoreType.DMA((n_lists,)),
        ],
        compiler_params=pltpu.CompilerParams(vmem_limit_bytes=VLIM * 1024 * 1024),
    )(
        me, *blocks, *[in_hbm(x) for x in (tile_counts, scale, offset)], vectors, in_hbm(codes)
    )


def where_kernel(p_ref, c_ref, hot_ref, row_ref):
    probes, cands = p_ref[...], c_ref[...]
    name = jnp.concatenate([probes[q : q + 1, :] for q in range(4)], axis=1)
    across = jnp.broadcast_to(name, (128, 128))
    earlier = iota((128, 128), 0) // 32 < iota((128, 128), 1) // 32
    rank = jnp.sum(jnp.where((across.T == across) & earlier, 1, 0), axis=0, keepdims=True)
    pairs = [(name // 4, (name % 4) * 2 + rank)]
    ids = [
        jnp.concatenate([cands[0:1, :], cands[1:2, :]], axis=1),
        jnp.concatenate([cands[2:3, :], cands[3:4, :]], axis=1),
    ]
    owner = [x // 1024 for x in ids]
    wide = [jnp.broadcast_to(x, (128, 128)) for x in owner]
    tall = [x.T for x in wide]
    before = iota((128, 128), 0) < iota((128, 128), 1)
    first = jnp.sum(jnp.where((tall[0] == wide[0]) & before, 1, 0), axis=0, keepdims=True)
    second = jnp.sum(jnp.where(tall[0] == wide[1], 1, 0), axis=0, keepdims=True) + jnp.sum(
        jnp.where((tall[1] == wide[1]) & before, 1, 0), axis=0, keepdims=True
    )
    pairs += [(owner[0], 8 + first), (owner[1], 8 + second)]
    for i, (holder, row) in enumerate(pairs):
        hot_ref[:, i * 128 : (i + 1) * 128] = (iota((128, 128), 0) == holder).astype(BF16)
        row_ref[:, i * 128 : (i + 1) * 128] = jnp.broadcast_to(row, (8, 128))


def where_to_look(probes, candidates):
    return pl.pallas_call(
        where_kernel,
        out_shape=(
            jax.ShapeDtypeStruct((128, 384), BF16),
            jax.ShapeDtypeStruct((8, 384), jnp.int32),
        ),
        in_specs=[vmem()] * 2,
        out_specs=(vmem(), vmem()),
        compiler_params=pltpu.CompilerParams(vmem_limit_bytes=4 * 1024 * 1024),
    )(probes, candidates)


def pick_kernel(got_ref, hot_ref, row_ref, best_ref, rerank_ref):
    got = got_ref[...].T[0:16, :]
    found = choose(got, hot_ref[...])
    mask = iota((16, 384), 0) == jnp.concatenate([row_ref[...], row_ref[...]], axis=0)
    vals = jnp.sum(jnp.where(mask, found, 0.0), axis=0, keepdims=True)
    best_ref[...] = jnp.concatenate([vals[:, q * 32 : (q + 1) * 32] for q in range(4)], axis=0)
    rerank_ref[...] = jnp.concatenate(
        [vals[:, 128 + q * 64 : 192 + q * 64] for q in range(4)], axis=0
    )


def pick(got, hot, row, probes, candidates):
    return pl.pallas_call(
        pick_kernel,
        out_shape=(
            jax.ShapeDtypeStruct(probes.shape, F32),
            jax.ShapeDtypeStruct(candidates.shape, F32),
        ),
        in_specs=[vmem()] * 3,
        out_specs=(vmem(), vmem()),
        compiler_params=pltpu.CompilerParams(vmem_limit_bytes=4 * 1024 * 1024),
    )(got, hot, row)


def place_of(at, core):
    return ((at["x"] * 4 + at["z"]) * 4 + at["y"]) * 2 + core


def chips():
    return [{"x": x, "z": z, "y": y} for x in range(4) for z in range(4) for y in range(4)]


def plane_groups(last):
    return [
        [place_of(at, core) for at in chips() if at[last[core]] == place]
        for core in range(2)
        for place in range(4)
    ]


def shift_pairs(step, last):
    pairs = []
    for at in chips():
        for core in range(2):
            to = dict(at)
            to[last[core]] = (at[last[core]] + step) % 4
            pairs.append((place_of(at, core), place_of(to, core)))
    return pairs


def other_core():
    return [(i, i ^ 1) for i in range(128)]


LAST = "zy"


def local(queries, probes, codes, scale, offset, tile_counts, raw_vectors, candidates):
    me = lax.axis_index(AXIS).astype(jnp.int32).reshape(1)
    copies = pack(me, queries, probes, candidates, 16)
    have = lax.all_to_all(
        copies, AXIS, split_axis=0, concat_axis=0, tiled=True, axis_index_groups=plane_groups(LAST)
    )
    blocks = [have] + [lax.ppermute(have, AXIS, shift_pairs(k, LAST)) for k in (1, 3, 2)]
    ours, vecs_in = fetch(have, raw_vectors)
    blocks = blocks + [lax.ppermute(b, AXIS, other_core()) for b in [ours] + blocks[1:]]
    found = score(me, tile_counts, blocks, scale, offset, vecs_in, codes)
    devices = found.shape[0]
    back = lax.all_to_all(found.reshape(devices, 1, 128), AXIS, split_axis=0, concat_axis=0, tiled=True)
    hot, row = where_to_look(probes, candidates)
    return pick(back.reshape(devices, 128), hot, row, probes, candidates)


def solution(mesh):
    flat = Mesh(mesh.devices.reshape(-1), (AXIS,))
    in_specs = (
        P(AXIS, None),
        P(AXIS, None),
        P(AXIS, None, None),
        P(AXIS, None),
        P(AXIS, None),
        P(AXIS),
        P(AXIS, None),
        P(AXIS, None),
    )
    out_specs = (P(AXIS, None), P(AXIS, None))
    return jax.shard_map(local, mesh=flat, in_specs=in_specs, out_specs=out_specs, check_vma=False)
```

```python
import functools

import jax
import jax.numpy as jnp
from jax import lax
from jax.experimental import pallas as pl
from jax.experimental.pallas import tpu as pltpu
from jax.sharding import Mesh, PartitionSpec as P

TILE = 256
AXIS = "device"
VLIM = 40
ROWS = 35
F32 = jnp.float32
BF16 = jnp.bfloat16
HIGH = lax.Precision.HIGHEST
NT = (((1,), (1,)), ((), ()))
NN = (((1,), (0,)), ((), ()))


def dot(a, b, dims=NN, precision=None):
    return lax.dot_general(a, b, dims, precision=precision, preferred_element_type=F32)


def iota(shape, dim):
    return lax.broadcasted_iota(jnp.int32, shape, dim)


def choose(values, hot):
    high = values.astype(BF16)
    rest = values - high.astype(F32)
    mid = rest.astype(BF16)
    low = (rest - mid.astype(F32)).astype(BF16)
    n = values.shape[0]
    out = dot(jnp.concatenate([high, mid, low], axis=0), hot)
    return out[:n] + out[n : 2 * n] + out[2 * n :]


def vmem():
    return pl.BlockSpec(memory_space=pltpu.VMEM)


def smem():
    return pl.BlockSpec(memory_space=pltpu.SMEM)


def in_hbm(x):
    return pltpu.with_memory_space_constraint(x, pltpu.HBM)


def hbm():
    return pl.BlockSpec(memory_space=pl.ANY)


def pack_kernel(q_hbm, p_hbm, c_hbm, out_ref, q_ref, p_ref, c_ref, sems):
    pairs = [(q_hbm, q_ref), (p_hbm, p_ref), (c_hbm, c_ref)]
    arrivals = [pltpu.make_async_copy(src, dst, sems.at[i]) for i, (src, dst) in enumerate(pairs)]
    for copy in arrivals:
        copy.start()
    for copy in arrivals:
        copy.wait()
    q_dev = q_ref.shape[0]
    queries = q_ref[...]
    rows = [queries[q : q + 1, c * 128 : (c + 1) * 128] for q in range(q_dev) for c in range(8)]
    probes = p_ref[...].astype(F32)
    rows.append(jnp.concatenate([probes[q : q + 1, :] for q in range(q_dev)], axis=1))
    cands = c_ref[...].astype(F32)
    rows.append(jnp.concatenate([cands[0:1, :], cands[1:2, :]], axis=1))
    rows.append(jnp.concatenate([cands[2:3, :], cands[3:4, :]], axis=1))
    packet = jnp.concatenate(rows, axis=0)
    for i in range(out_ref.shape[0] // ROWS):
        out_ref[i * ROWS : (i + 1) * ROWS, :] = packet


def pack(queries, probes, candidates, copies):
    return pl.pallas_call(
        pack_kernel,
        out_shape=jax.ShapeDtypeStruct((copies * ROWS, 128), F32),
        in_specs=[hbm()] * 3,
        out_specs=vmem(),
        scratch_shapes=[pltpu.VMEM(x.shape, x.dtype) for x in (queries, probes, candidates)]
        + [pltpu.SemaphoreType.DMA((3,))],
        compiler_params=pltpu.CompilerParams(vmem_limit_bytes=8 * 1024 * 1024),
    )(*[in_hbm(x) for x in (queries, probes, candidates)])


def score_kernel(me_ref, *refs, n_blocks, n_lists, n_rows, v_dev):
    blocks = refs[:n_blocks]
    tiles_hbm, scale_hbm, offset_hbm, vecs_hbm, codes_hbm, out_ref = refs[n_blocks : n_blocks + 6]
    (
        tiles_ref, scale_ref, offset_ref, codes_ref, vecs_ref,
        fold, base_acc, prod, spot_v, spot_s, sem, small_sems, vec_sems, code_sems,
    ) = refs[n_blocks + 6 :]
    me = me_ref[0]
    code_copies = [
        pltpu.make_async_copy(codes_hbm.at[l], codes_ref.at[l], code_sems.at[l])
        for l in range(n_lists)
    ]
    vec_copies = [
        pltpu.make_async_copy(
            vecs_hbm.at[:, pl.ds(c * 128, 128)], vecs_ref.at[:, c, :], vec_sems.at[c]
        )
        for c in range(8)
    ]
    small_copies = [
        pltpu.make_async_copy(src, dst, small_sems.at[i])
        for i, (src, dst) in enumerate(
            [(scale_hbm, scale_ref), (offset_hbm, offset_ref), (tiles_hbm, tiles_ref)]
        )
    ]
    for copy in small_copies + vec_copies + code_copies[:1]:
        copy.start()
    n_tiles = n_rows // TILE
    per = blocks[0].shape[0] // ROWS
    dev = n_blocks * per

    def rows_of(r):
        return jnp.concatenate([b[pl.ds(r, per, stride=ROWS), :] for b in blocks], axis=0)

    core, mine_y, mine_z = me % 2, me // 2 % 4, me // 8 % 4
    major, minor = iota((per, 128), 0) // 4, iota((per, 128), 0) % 4
    names = []
    for b in range(n_blocks):
        step = SHIFTS[b % 4]
        from_core = core if b < n_blocks // 2 else 1 - core
        by_z = (major * 4 + (mine_z + 4 - step) % 4) * 4 + minor
        by_y = (major * 4 + minor) * 4 + (mine_y + 4 - step) % 4
        names.append(jnp.where(from_core == 0, by_z, by_y) * 2 + from_core)
    ident = jnp.concatenate(names, axis=0)

    cand = jnp.concatenate([rows_of(33), rows_of(34)], axis=1).astype(jnp.int32)
    local_id = cand - me * v_dev
    mine = (local_id >= 0) & (local_id < v_dev)
    tri = (iota((256, 256), 0) < iota((256, 256), 1)).astype(BF16)
    rank = dot(mine.astype(BF16), tri)
    place = local_id + iota((dev, 256), 1) // 64 * v_dev
    high = (place // 64).astype(F32)
    low = (place % 64).astype(F32)
    one = jnp.ones((8, 256), BF16)
    spots = []
    for k in range(4):
        here = mine & (rank == float(k))
        hi = dot(one, jnp.where(here, high, 0.0).astype(BF16), NT)
        lo = dot(one, jnp.where(here, low, 0.0).astype(BF16), NT)
        spots.append((hi[0:1, :] * 64.0 + lo[0:1, :]).astype(jnp.int32))
    first_row = iota((1, dev), 1) % per * ROWS
    spot_v[...] = jnp.concatenate(
        [x % v_dev for x in spots] + [x // v_dev * 8 + first_row for x in spots], axis=0
    )
    to_smem = pltpu.make_async_copy(spot_v, spot_s, sem)
    to_smem.start()

    probe = rows_of(32)
    eq = jnp.concatenate(
        [(probe == (me * n_lists + l).astype(F32)).astype(BF16) for l in range(n_lists)], axis=0
    )
    seg = (iota((128, 384), 0) // 32 == iota((128, 384), 1) // 128).astype(BF16)
    hits = dot(eq, seg)
    perm = (ident == iota((dev, 128), 1)).astype(F32).astype(BF16)

    for copy in small_copies:
        copy.wait()
    code_copies[1].start()
    for b in range(n_blocks):
        r0 = b * per
        if b == 4:
            code_copies[2].start()
        for l in range(n_lists):
            h = [hits[l * dev + r0 : l * dev + r0 + per, q * 128 : (q + 1) * 128] for q in range(3)]
            m0, m1, m2 = h[0] > 0.5, h[1] > 0.5, h[2] > 0.5
            s1 = (h[0] + h[1]) > 1.5
            s2 = (h[0] + h[1] + h[2]) > 1.5
            acc = [None, None]
            for c in range(8):
                x = [blocks[b][pl.ds(q * 8 + c, per, stride=ROWS), :] for q in range(4)]
                first = jnp.where(m0, x[0], jnp.where(m1, x[1], jnp.where(m2, x[2], x[3])))
                second = jnp.where(s1, x[1], jnp.where(s2, x[2], x[3]))
                sc = scale_ref[l : l + 1, c * 128 : (c + 1) * 128]
                of = offset_ref[l : l + 1, c * 128 : (c + 1) * 128]
                for s, take in enumerate((first, second)):
                    fold[l, s * dev + r0 : s * dev + r0 + per, c * 128 : (c + 1) * 128] = (
                        take * sc
                    ).astype(BF16)
                    part = take * of
                    acc[s] = part if acc[s] is None else acc[s] + part
            for s in range(2):
                base_acc[l, s * dev + r0 : s * dev + r0 + per, :] = acc[s]

    to_smem.wait()
    for copy in vec_copies:
        copy.wait()
    code_copies[3].start()

    def gather(part):
        for j in range(part * 4, part * 4 + 4):
            b = j // per
            for k in range(4):
                row, q = spot_s[k, j], spot_s[4 + k, j]
                to = (k * dev + j) * 8
                prod[to : to + 8, :] = vecs_ref[row] * blocks[b][pl.ds(q, 8), :]

    out_rows = []
    steps = n_lists * n_tiles
    done = 0
    for l in range(n_lists):
        folded = fold[l]
        code_copies[l].wait()
        best = None
        for t in range(n_tiles):
            s = dot(codes_ref[l, t * TILE : (t + 1) * TILE, :], folded, NT)
            m = jnp.max(s.reshape(TILE // 8, 8, 2 * dev), axis=0)
            if t == 0:
                best = m
            else:
                best = jnp.where(t < tiles_ref[l], jnp.maximum(best, m), best)
            if (l * n_tiles + t + 1) * (dev // 4) // steps > done:
                gather(done)
                done += 1
        best = jnp.max(best, axis=0, keepdims=True)
        for s in range(2):
            base = base_acc[l, s * dev : (s + 1) * dev, :].T
            out_rows.append(best[:, s * dev : (s + 1) * dev] + jnp.sum(base, axis=0, keepdims=True))
    for k in range(4):
        total = None
        for c in range(8):
            x = prod[pl.ds(k * dev * 8 + c, dev, stride=8), :]
            total = x if total is None else total + x
        out_rows.append(jnp.sum(total.T, axis=0, keepdims=True))
    pad = jnp.zeros((16 - len(out_rows), dev), F32)
    table = jnp.concatenate(out_rows + [pad], axis=0)
    table = choose(table, perm)
    table = jnp.concatenate([table, jnp.zeros((112, 128), F32)], axis=0)
    out_ref[...] = table.T


def score(me, tile_counts, blocks, scale, offset, vectors, codes):
    n_lists, n_rows, width = codes.shape
    v_dev = vectors.shape[0]
    per = blocks[0].shape[0] // ROWS
    dev = per * len(blocks)
    body = functools.partial(
        score_kernel, n_blocks=len(blocks), n_lists=n_lists, n_rows=n_rows, v_dev=v_dev
    )
    return pl.pallas_call(
        body,
        out_shape=jax.ShapeDtypeStruct((dev, 128), F32),
        in_specs=[smem()] + [vmem()] * len(blocks) + [hbm()] * 5,
        out_specs=vmem(),
        scratch_shapes=[
            pltpu.SMEM(tile_counts.shape, jnp.int32),
            pltpu.VMEM(scale.shape, F32),
            pltpu.VMEM(offset.shape, F32),
            pltpu.VMEM(codes.shape, BF16),
            pltpu.VMEM((v_dev, 8, 128), F32),
            pltpu.VMEM((n_lists, 2 * dev, width), BF16),
            pltpu.VMEM((n_lists, 2 * dev, 128), F32),
            pltpu.VMEM((4 * dev * 8, 128), F32),
            pltpu.VMEM((8, dev), jnp.int32),
            pltpu.SMEM((8, dev), jnp.int32),
            pltpu.SemaphoreType.DMA,
            pltpu.SemaphoreType.DMA((3,)),
            pltpu.SemaphoreType.DMA((8,)),
            pltpu.SemaphoreType.DMA((n_lists,)),
        ],
        compiler_params=pltpu.CompilerParams(vmem_limit_bytes=VLIM * 1024 * 1024),
    )(
        me, *blocks, *[in_hbm(x) for x in (tile_counts, scale, offset, vectors, codes)]
    )


def where_kernel(p_ref, c_ref, hot_ref, row_ref):
    probes, cands = p_ref[...], c_ref[...]
    name = jnp.concatenate([probes[q : q + 1, :] for q in range(4)], axis=1)
    across = jnp.broadcast_to(name, (128, 128))
    earlier = iota((128, 128), 0) // 32 < iota((128, 128), 1) // 32
    rank = jnp.sum(jnp.where((across.T == across) & earlier, 1, 0), axis=0, keepdims=True)
    pairs = [(name // 4, (name % 4) * 2 + rank)]
    ids = [
        jnp.concatenate([cands[0:1, :], cands[1:2, :]], axis=1),
        jnp.concatenate([cands[2:3, :], cands[3:4, :]], axis=1),
    ]
    owner = [x // 1024 for x in ids]
    wide = [jnp.broadcast_to(x, (128, 128)) for x in owner]
    tall = [x.T for x in wide]
    before = iota((128, 128), 0) < iota((128, 128), 1)
    first = jnp.sum(jnp.where((tall[0] == wide[0]) & before, 1, 0), axis=0, keepdims=True)
    second = jnp.sum(jnp.where(tall[0] == wide[1], 1, 0), axis=0, keepdims=True) + jnp.sum(
        jnp.where((tall[1] == wide[1]) & before, 1, 0), axis=0, keepdims=True
    )
    pairs += [(owner[0], 8 + first), (owner[1], 8 + second)]
    for i, (holder, row) in enumerate(pairs):
        hot_ref[:, i * 128 : (i + 1) * 128] = (iota((128, 128), 0) == holder).astype(BF16)
        row_ref[:, i * 128 : (i + 1) * 128] = jnp.broadcast_to(row, (8, 128))


def where_to_look(probes, candidates):
    return pl.pallas_call(
        where_kernel,
        out_shape=(
            jax.ShapeDtypeStruct((128, 384), BF16),
            jax.ShapeDtypeStruct((8, 384), jnp.int32),
        ),
        in_specs=[vmem()] * 2,
        out_specs=(vmem(), vmem()),
        compiler_params=pltpu.CompilerParams(vmem_limit_bytes=4 * 1024 * 1024),
    )(probes, candidates)


def pick_kernel(got_ref, hot_ref, row_ref, best_ref, rerank_ref):
    got = got_ref[...].T[0:16, :]
    found = choose(got, hot_ref[...])
    mask = iota((16, 384), 0) == jnp.concatenate([row_ref[...], row_ref[...]], axis=0)
    vals = jnp.sum(jnp.where(mask, found, 0.0), axis=0, keepdims=True)
    best_ref[...] = jnp.concatenate([vals[:, q * 32 : (q + 1) * 32] for q in range(4)], axis=0)
    rerank_ref[...] = jnp.concatenate(
        [vals[:, 128 + q * 64 : 192 + q * 64] for q in range(4)], axis=0
    )


def pick(got, hot, row, probes, candidates):
    return pl.pallas_call(
        pick_kernel,
        out_shape=(
            jax.ShapeDtypeStruct(probes.shape, F32),
            jax.ShapeDtypeStruct(candidates.shape, F32),
        ),
        in_specs=[vmem()] * 3,
        out_specs=(vmem(), vmem()),
        compiler_params=pltpu.CompilerParams(vmem_limit_bytes=4 * 1024 * 1024),
    )(got, hot, row)


def place_of(at, core):
    return ((at["x"] * 4 + at["z"]) * 4 + at["y"]) * 2 + core


def chips():
    return [{"x": x, "z": z, "y": y} for x in range(4) for z in range(4) for y in range(4)]


def plane_groups(last):
    return [
        [place_of(at, core) for at in chips() if at[last[core]] == place]
        for core in range(2)
        for place in range(4)
    ]


def shift_pairs(step, last):
    pairs = []
    for at in chips():
        for core in range(2):
            to = dict(at)
            to[last[core]] = (at[last[core]] + step) % 4
            pairs.append((place_of(at, core), place_of(to, core)))
    return pairs


def other_core():
    return [(i, i ^ 1) for i in range(128)]


LAST = "zy"
SHIFTS = (0, 1, 3, 2)


def local(queries, probes, codes, scale, offset, tile_counts, raw_vectors, candidates):
    me = lax.axis_index(AXIS).astype(jnp.int32).reshape(1)
    copies = pack(queries, probes, candidates, 16)
    have = lax.all_to_all(
        copies.reshape(16, 1, ROWS * 128), AXIS, split_axis=0, concat_axis=0, tiled=True, axis_index_groups=plane_groups(LAST)
    ).reshape(16 * ROWS, 128)
    blocks = [have] + [lax.ppermute(have, AXIS, shift_pairs(k, LAST)) for k in SHIFTS[1:]]
    blocks = blocks + [lax.ppermute(b, AXIS, other_core()) for b in blocks]
    found = score(me, tile_counts, blocks, scale, offset, raw_vectors, codes)
    devices = found.shape[0]
    back = lax.all_to_all(found.reshape(devices, 1, 128), AXIS, split_axis=0, concat_axis=0, tiled=True)
    hot, row = where_to_look(probes, candidates)
    return pick(back.reshape(devices, 128), hot, row, probes, candidates)


def solution(mesh):
    flat = Mesh(mesh.devices.reshape(-1), (AXIS,))
    in_specs = (
        P(AXIS, None),
        P(AXIS, None),
        P(AXIS, None, None),
        P(AXIS, None),
        P(AXIS, None),
        P(AXIS),
        P(AXIS, None),
        P(AXIS, None),
    )
    out_specs = (P(AXIS, None), P(AXIS, None))
    return jax.shard_map(local, mesh=flat, in_specs=in_specs, out_specs=out_specs, check_vma=False)
```

```python
import functools

import jax
import jax.numpy as jnp
from jax import lax
from jax.experimental import pallas as pl
from jax.experimental.pallas import tpu as pltpu
from jax.sharding import Mesh, PartitionSpec as P

TILE = 256
AXIS = "device"
VLIM = 40
ROWS = 35
F32 = jnp.float32
BF16 = jnp.bfloat16
HIGH = lax.Precision.HIGHEST
NT = (((1,), (1,)), ((), ()))
NN = (((1,), (0,)), ((), ()))


def dot(a, b, dims=NN, precision=None):
    return lax.dot_general(a, b, dims, precision=precision, preferred_element_type=F32)


def iota(shape, dim):
    return lax.broadcasted_iota(jnp.int32, shape, dim)


def choose(values, hot):
    high = values.astype(BF16)
    rest = values - high.astype(F32)
    mid = rest.astype(BF16)
    low = (rest - mid.astype(F32)).astype(BF16)
    n = values.shape[0]
    out = dot(jnp.concatenate([high, mid, low], axis=0), hot)
    return out[:n] + out[n : 2 * n] + out[2 * n :]


def vmem():
    return pl.BlockSpec(memory_space=pltpu.VMEM)


def smem():
    return pl.BlockSpec(memory_space=pltpu.SMEM)


def in_hbm(x):
    return pltpu.with_memory_space_constraint(x, pltpu.HBM)


def hbm():
    return pl.BlockSpec(memory_space=pl.ANY)


def pack_kernel(q_hbm, p_hbm, c_hbm, out_ref, q_ref, p_ref, c_ref, sems):
    pairs = [(q_hbm, q_ref), (p_hbm, p_ref), (c_hbm, c_ref)]
    arrivals = [pltpu.make_async_copy(src, dst, sems.at[i]) for i, (src, dst) in enumerate(pairs)]
    for copy in arrivals:
        copy.start()
    for copy in arrivals:
        copy.wait()
    q_dev = q_ref.shape[0]
    queries = q_ref[...]
    rows = [queries[q : q + 1, c * 128 : (c + 1) * 128] for q in range(q_dev) for c in range(8)]
    probes = p_ref[...].astype(F32)
    rows.append(jnp.concatenate([probes[q : q + 1, :] for q in range(q_dev)], axis=1))
    cands = c_ref[...].astype(F32)
    rows.append(jnp.concatenate([cands[0:1, :], cands[1:2, :]], axis=1))
    rows.append(jnp.concatenate([cands[2:3, :], cands[3:4, :]], axis=1))
    packet = jnp.concatenate(rows, axis=0)
    for i in range(out_ref.shape[0] // ROWS):
        out_ref[i * ROWS : (i + 1) * ROWS, :] = packet


def pack(queries, probes, candidates, copies):
    return pl.pallas_call(
        pack_kernel,
        out_shape=jax.ShapeDtypeStruct((copies * ROWS, 128), F32),
        in_specs=[hbm()] * 3,
        out_specs=vmem(),
        scratch_shapes=[pltpu.VMEM(x.shape, x.dtype) for x in (queries, probes, candidates)]
        + [pltpu.SemaphoreType.DMA((3,))],
        compiler_params=pltpu.CompilerParams(vmem_limit_bytes=8 * 1024 * 1024),
    )(*[in_hbm(x) for x in (queries, probes, candidates)])


def score_kernel(me_ref, *refs, n_blocks, n_lists, n_rows, v_dev):
    blocks = refs[:n_blocks]
    tiles_hbm, scale_hbm, offset_hbm, vecs_hbm, codes_hbm, out_ref = refs[n_blocks : n_blocks + 6]
    (
        tiles_ref, scale_ref, offset_ref, codes_ref, vecs_ref,
        fold, base_acc, prod, spot_v, spot_s, sem, small_sems, vec_sems, code_sems,
    ) = refs[n_blocks + 6 :]
    me = me_ref[0]
    code_copies = [
        pltpu.make_async_copy(codes_hbm.at[l], codes_ref.at[l], code_sems.at[l])
        for l in range(n_lists)
    ]
    vec_copies = [
        pltpu.make_async_copy(
            vecs_hbm.at[:, pl.ds(c * 128, 128)], vecs_ref.at[:, c, :], vec_sems.at[c]
        )
        for c in range(8)
    ]
    small_copies = [
        pltpu.make_async_copy(src, dst, small_sems.at[i])
        for i, (src, dst) in enumerate(
            [(scale_hbm, scale_ref), (offset_hbm, offset_ref), (tiles_hbm, tiles_ref)]
        )
    ]
    for copy in small_copies + code_copies[:1]:
        copy.start()
    n_tiles = n_rows // TILE
    per = blocks[0].shape[0] // ROWS
    dev = n_blocks * per

    def rows_of(r):
        return jnp.concatenate([b[pl.ds(r, per, stride=ROWS), :] for b in blocks], axis=0)

    core, mine_y, mine_z = me % 2, me // 2 % 4, me // 8 % 4
    major, minor = iota((per, 128), 0) // 4, iota((per, 128), 0) % 4
    names = []
    for b in range(n_blocks):
        step = SHIFTS[b % 4]
        from_core = core if b < n_blocks // 2 else 1 - core
        by_z = (major * 4 + (mine_z + 4 - step) % 4) * 4 + minor
        by_y = (major * 4 + minor) * 4 + (mine_y + 4 - step) % 4
        names.append(jnp.where(from_core == 0, by_z, by_y) * 2 + from_core)
    ident = jnp.concatenate(names, axis=0)

    cand = jnp.concatenate([rows_of(33), rows_of(34)], axis=1).astype(jnp.int32)
    local_id = cand - me * v_dev
    mine = (local_id >= 0) & (local_id < v_dev)
    tri = (iota((256, 256), 0) < iota((256, 256), 1)).astype(BF16)
    rank = dot(mine.astype(BF16), tri)
    place = local_id + iota((dev, 256), 1) // 64 * v_dev
    high = (place // 64).astype(F32)
    low = (place % 64).astype(F32)
    one = jnp.ones((8, 256), BF16)
    spots = []
    for k in range(4):
        here = mine & (rank == float(k))
        hi = dot(one, jnp.where(here, high, 0.0).astype(BF16), NT)
        lo = dot(one, jnp.where(here, low, 0.0).astype(BF16), NT)
        spots.append((hi[0:1, :] * 64.0 + lo[0:1, :]).astype(jnp.int32))
    first_row = iota((1, dev), 1) % per * ROWS
    spot_v[...] = jnp.concatenate(
        [x % v_dev for x in spots] + [x // v_dev * 8 + first_row for x in spots], axis=0
    )
    to_smem = pltpu.make_async_copy(spot_v, spot_s, sem)
    to_smem.start()

    probe = rows_of(32)
    eq = jnp.concatenate(
        [(probe == (me * n_lists + l).astype(F32)).astype(BF16) for l in range(n_lists)], axis=0
    )
    seg = (iota((128, 384), 0) // 32 == iota((128, 384), 1) // 128).astype(BF16)
    hits = dot(eq, seg)
    perm = (ident == iota((dev, 128), 1)).astype(F32).astype(BF16)

    for copy in small_copies:
        copy.wait()
    for copy in [code_copies[1]] + vec_copies:
        copy.start()
    for b in range(n_blocks):
        r0 = b * per
        if b == 4:
            code_copies[2].start()
        for l in range(n_lists):
            h = [hits[l * dev + r0 : l * dev + r0 + per, q * 128 : (q + 1) * 128] for q in range(3)]
            m0, m1, m2 = h[0] > 0.5, h[1] > 0.5, h[2] > 0.5
            s1 = (h[0] + h[1]) > 1.5
            s2 = (h[0] + h[1] + h[2]) > 1.5
            acc = [None, None]
            for c in range(8):
                x = [blocks[b][pl.ds(q * 8 + c, per, stride=ROWS), :] for q in range(4)]
                first = jnp.where(m0, x[0], jnp.where(m1, x[1], jnp.where(m2, x[2], x[3])))
                second = jnp.where(s1, x[1], jnp.where(s2, x[2], x[3]))
                sc = scale_ref[l : l + 1, c * 128 : (c + 1) * 128]
                of = offset_ref[l : l + 1, c * 128 : (c + 1) * 128]
                for s, take in enumerate((first, second)):
                    fold[l, s * dev + r0 : s * dev + r0 + per, c * 128 : (c + 1) * 128] = (
                        take * sc
                    ).astype(BF16)
                    part = take * of
                    acc[s] = part if acc[s] is None else acc[s] + part
            for s in range(2):
                base_acc[l, s * dev + r0 : s * dev + r0 + per, :] = acc[s]

    to_smem.wait()
    code_copies[3].start()

    def gather(part):
        for j in range(part * 4, part * 4 + 4):
            b = j // per
            for k in range(4):
                row, q = spot_s[k, j], spot_s[4 + k, j]
                to = (k * dev + j) * 8
                prod[to : to + 8, :] = vecs_ref[row] * blocks[b][pl.ds(q, 8), :]

    out_rows = []
    steps = n_lists * n_tiles
    done = 0
    for l in range(n_lists):
        folded = fold[l]
        code_copies[l].wait()
        if l == n_lists // 2:
            for copy in vec_copies:
                copy.wait()
        best = None
        for t in range(n_tiles):
            s = dot(codes_ref[l, t * TILE : (t + 1) * TILE, :], folded, NT)
            m = jnp.max(s.reshape(TILE // 8, 8, 2 * dev), axis=0)
            if t == 0:
                best = m
            else:
                best = jnp.where(t < tiles_ref[l], jnp.maximum(best, m), best)
            due = (2 * (l * n_tiles + t + 1) - steps) * (dev // 4) // steps
            while done < due:
                gather(done)
                done += 1
        best = jnp.max(best, axis=0, keepdims=True)
        for s in range(2):
            base = base_acc[l, s * dev : (s + 1) * dev, :].T
            out_rows.append(best[:, s * dev : (s + 1) * dev] + jnp.sum(base, axis=0, keepdims=True))
    for k in range(4):
        total = None
        for c in range(8):
            x = prod[pl.ds(k * dev * 8 + c, dev, stride=8), :]
            total = x if total is None else total + x
        out_rows.append(jnp.sum(total.T, axis=0, keepdims=True))
    pad = jnp.zeros((16 - len(out_rows), dev), F32)
    table = jnp.concatenate(out_rows + [pad], axis=0)
    table = choose(table, perm)
    table = jnp.concatenate([table, jnp.zeros((112, 128), F32)], axis=0)
    out_ref[...] = table.T


def score(me, tile_counts, blocks, scale, offset, vectors, codes):
    n_lists, n_rows, width = codes.shape
    v_dev = vectors.shape[0]
    per = blocks[0].shape[0] // ROWS
    dev = per * len(blocks)
    body = functools.partial(
        score_kernel, n_blocks=len(blocks), n_lists=n_lists, n_rows=n_rows, v_dev=v_dev
    )
    return pl.pallas_call(
        body,
        out_shape=jax.ShapeDtypeStruct((dev, 128), F32),
        in_specs=[smem()] + [vmem()] * len(blocks) + [hbm()] * 5,
        out_specs=vmem(),
        scratch_shapes=[
            pltpu.SMEM(tile_counts.shape, jnp.int32),
            pltpu.VMEM(scale.shape, F32),
            pltpu.VMEM(offset.shape, F32),
            pltpu.VMEM(codes.shape, BF16),
            pltpu.VMEM((v_dev, 8, 128), F32),
            pltpu.VMEM((n_lists, 2 * dev, width), BF16),
            pltpu.VMEM((n_lists, 2 * dev, 128), F32),
            pltpu.VMEM((4 * dev * 8, 128), F32),
            pltpu.VMEM((8, dev), jnp.int32),
            pltpu.SMEM((8, dev), jnp.int32),
            pltpu.SemaphoreType.DMA,
            pltpu.SemaphoreType.DMA((3,)),
            pltpu.SemaphoreType.DMA((8,)),
            pltpu.SemaphoreType.DMA((n_lists,)),
        ],
        compiler_params=pltpu.CompilerParams(vmem_limit_bytes=VLIM * 1024 * 1024),
    )(
        me, *blocks, *[in_hbm(x) for x in (tile_counts, scale, offset, vectors, codes)]
    )


def where_kernel(p_ref, c_ref, hot_ref, row_ref):
    probes, cands = p_ref[...], c_ref[...]
    name = jnp.concatenate([probes[q : q + 1, :] for q in range(4)], axis=1)
    across = jnp.broadcast_to(name, (128, 128))
    earlier = iota((128, 128), 0) // 32 < iota((128, 128), 1) // 32
    rank = jnp.sum(jnp.where((across.T == across) & earlier, 1, 0), axis=0, keepdims=True)
    pairs = [(name // 4, (name % 4) * 2 + rank)]
    ids = [
        jnp.concatenate([cands[0:1, :], cands[1:2, :]], axis=1),
        jnp.concatenate([cands[2:3, :], cands[3:4, :]], axis=1),
    ]
    owner = [x // 1024 for x in ids]
    wide = [jnp.broadcast_to(x, (128, 128)) for x in owner]
    tall = [x.T for x in wide]
    before = iota((128, 128), 0) < iota((128, 128), 1)
    first = jnp.sum(jnp.where((tall[0] == wide[0]) & before, 1, 0), axis=0, keepdims=True)
    second = jnp.sum(jnp.where(tall[0] == wide[1], 1, 0), axis=0, keepdims=True) + jnp.sum(
        jnp.where((tall[1] == wide[1]) & before, 1, 0), axis=0, keepdims=True
    )
    pairs += [(owner[0], 8 + first), (owner[1], 8 + second)]
    for i, (holder, row) in enumerate(pairs):
        hot_ref[:, i * 128 : (i + 1) * 128] = (iota((128, 128), 0) == holder).astype(BF16)
        row_ref[:, i * 128 : (i + 1) * 128] = jnp.broadcast_to(row, (8, 128))


def where_to_look(probes, candidates):
    return pl.pallas_call(
        where_kernel,
        out_shape=(
            jax.ShapeDtypeStruct((128, 384), BF16),
            jax.ShapeDtypeStruct((8, 384), jnp.int32),
        ),
        in_specs=[vmem()] * 2,
        out_specs=(vmem(), vmem()),
        compiler_params=pltpu.CompilerParams(vmem_limit_bytes=4 * 1024 * 1024),
    )(probes, candidates)


def pick_kernel(got_ref, hot_ref, row_ref, best_ref, rerank_ref):
    got = got_ref[...].T[0:16, :]
    found = choose(got, hot_ref[...])
    mask = iota((16, 384), 0) == jnp.concatenate([row_ref[...], row_ref[...]], axis=0)
    vals = jnp.sum(jnp.where(mask, found, 0.0), axis=0, keepdims=True)
    best_ref[...] = jnp.concatenate([vals[:, q * 32 : (q + 1) * 32] for q in range(4)], axis=0)
    rerank_ref[...] = jnp.concatenate(
        [vals[:, 128 + q * 64 : 192 + q * 64] for q in range(4)], axis=0
    )


def pick(got, hot, row, probes, candidates):
    return pl.pallas_call(
        pick_kernel,
        out_shape=(
            jax.ShapeDtypeStruct(probes.shape, F32),
            jax.ShapeDtypeStruct(candidates.shape, F32),
        ),
        in_specs=[vmem()] * 3,
        out_specs=(vmem(), vmem()),
        compiler_params=pltpu.CompilerParams(vmem_limit_bytes=4 * 1024 * 1024),
    )(got, hot, row)


def place_of(at, core):
    return ((at["x"] * 4 + at["z"]) * 4 + at["y"]) * 2 + core


def chips():
    return [{"x": x, "z": z, "y": y} for x in range(4) for z in range(4) for y in range(4)]


def plane_groups(last):
    return [
        [place_of(at, core) for at in chips() if at[last[core]] == place]
        for core in range(2)
        for place in range(4)
    ]


def shift_pairs(step, last):
    pairs = []
    for at in chips():
        for core in range(2):
            to = dict(at)
            to[last[core]] = (at[last[core]] + step) % 4
            pairs.append((place_of(at, core), place_of(to, core)))
    return pairs


def other_core():
    return [(i, i ^ 1) for i in range(128)]


LAST = "zy"
SHIFTS = (0, 1, 3, 2)


def local(queries, probes, codes, scale, offset, tile_counts, raw_vectors, candidates):
    me = lax.axis_index(AXIS).astype(jnp.int32).reshape(1)
    copies = pack(queries, probes, candidates, 16)
    have = lax.all_to_all(
        copies.reshape(16, 1, ROWS * 128), AXIS, split_axis=0, concat_axis=0, tiled=True, axis_index_groups=plane_groups(LAST)
    ).reshape(16 * ROWS, 128)
    blocks = [have] + [lax.ppermute(have, AXIS, shift_pairs(k, LAST)) for k in SHIFTS[1:]]
    blocks = blocks + [lax.ppermute(b, AXIS, other_core()) for b in blocks]
    found = score(me, tile_counts, blocks, scale, offset, raw_vectors, codes)
    devices = found.shape[0]
    back = lax.all_to_all(found.reshape(devices, 1, 128), AXIS, split_axis=0, concat_axis=0, tiled=True)
    hot, row = where_to_look(probes, candidates)
    return pick(back.reshape(devices, 128), hot, row, probes, candidates)


def solution(mesh):
    flat = Mesh(mesh.devices.reshape(-1), (AXIS,))
    in_specs = (
        P(AXIS, None),
        P(AXIS, None),
        P(AXIS, None, None),
        P(AXIS, None),
        P(AXIS, None),
        P(AXIS),
        P(AXIS, None),
        P(AXIS, None),
    )
    out_specs = (P(AXIS, None), P(AXIS, None))
    return jax.shard_map(local, mesh=flat, in_specs=in_specs, out_specs=out_specs, check_vma=False)
```
